1024 devices in a mesh: wave: 32 (over x, y, core), lev: 32 (over z).
Axes of the slice: x: 4, y: 4, z: 32, core: 2. Of those that a mesh axis runs over, the one named last changes fastest.
Arguments:
- spectral: bfloat16 [2, 32, 2, 32, 1280], P(None, 'lev', None, 'wave'), may hold values from -6 to 6
- legendre: bfloat16 [32, 2560, 1280], P('wave'), may hold values from -0.15625 to 0.15625
- wavenumber: int32 [32], replicated, may hold values from 0 to 1279, as said below
Outputs:
- tendency_spec: bfloat16 [2, 32, 2, 32, 1280], P(None, 'lev', None, 'wave')
The draws below stay inside these ranges and needn't reach their ends.
Inputs may be any that keep to these rules, and one draw needn't show every extreme that they name: `wavenumber`: distinct zonal wavenumbers; 0 and 1279 are always among them.
All inputs are finite; a program needn't handle non-finite values.
Results may differ from the reference program's by a relative error of at most 0.006.
Values may be sent and summed in bfloat16 or wider, within the bound.
A program may use at most 64 MiB of HBM per device.

```python
import math
import jax
import jax.numpy as jnp
from jax import lax

TRUNC = 1279
NLAT = 2560
NN = 1280
LEVELS = 32
MW = 32
LS = 80
BC = 161
N_WAVE = 32
N_LEV = 32


def draw_wavenumber(key, part):
    inner = jax.random.permutation(jax.random.fold_in(key, 11), TRUNC - 1).astype(jnp.int32) + 1
    picked = jnp.concatenate([jnp.array([0, TRUNC], dtype=jnp.int32), inner[:MW - 2]])
    return jax.random.permutation(jax.random.fold_in(key, 23), picked).astype(jnp.int32)


def steps_of(own_key, dims, cuts, smallest, top_value):
    factor_of = 1.0
    for position, blocks in cuts:
        steps = jax.random.uniform(jax.random.fold_in(jax.random.fold_in(own_key, 6), position), (blocks,), jnp.float32, smallest / len(cuts), top_value / len(cuts))
        factor_of = factor_of * jnp.repeat(jnp.exp(steps), dims[position] // blocks).reshape((-1,) + (1,) * (len(dims) - 1 - position))
    return factor_of


def gaussian(stream_key, extent, deviation, reach, cuts=(), kind=jnp.bfloat16):
    gain = steps_of(stream_key, extent, cuts, -0.22, 0.18) if cuts else 1.0
    values = jax.random.normal(stream_key, extent, jnp.float32) * deviation * gain
    return jnp.minimum(jnp.maximum(values, -reach), reach).astype(kind)


def setup_inputs(seed: int = 0) -> dict:
    splits = jax.random.split(jax.random.key(seed), 4)
    return {
        "spectral": gaussian(splits[0], (2, LEVELS, 2, MW, NN), 1.0, 6.0, ((1, 32), (3, 32))),
        "legendre": gaussian(splits[1], (MW, NLAT, NN), NN ** -0.5, 0.15625, ((0, 32),)),
        "wavenumber": draw_wavenumber(jax.random.fold_in(splits[3], 71), 0),
    }


def circle_tables(latitude, band_index, wavenumber, lat_total, band_total, band_cap, wave_total):
    circle_length = 20 + 4 * jnp.minimum(latitude, lat_total - 1 - latitude)
    band_width = (circle_length + band_total - 1) // band_total
    offsets = jnp.arange(band_cap, dtype=jnp.int32)
    longitude_index = band_index[None, :, None] * band_width[:, None, None] + offsets[None, None, :]
    inside = (offsets[None, None, :] < band_width[:, None, None]) & (longitude_index < circle_length[:, None, None])
    rows = latitude.shape[0]
    longitude_index = longitude_index.reshape(rows, -1)
    inside = inside.reshape(rows, -1)
    phase_index = wavenumber[None, None, :] * longitude_index[:, :, None] % circle_length[:, None, None]
    length_float = circle_length.astype(jnp.float32)
    angles = 2.0 * math.pi * phase_index.astype(jnp.float32) / length_float[:, None, None]
    shown = inside[:, :, None].astype(jnp.float32)
    trig_basis = jnp.stack([jnp.cos(angles) * shown, -jnp.sin(angles) * shown], axis=2)
    colatitude = (latitude.astype(jnp.float32) + 0.5) * (math.pi / lat_total)
    circle_weight = jnp.sin(colatitude) / jnp.sqrt(length_float)
    synth_table = (trig_basis / math.sqrt(wave_total)).astype(jnp.bfloat16)
    analysis_table = (trig_basis * circle_weight[:, None, None, None]).astype(jnp.bfloat16)
    return (synth_table, analysis_table, 2.0 * jnp.cos(colatitude))

def tendencies(grid_values, planetary):
    vorticity = grid_values[0]
    divergence = grid_values[1]
    absolute_vort = vorticity + planetary[None, :, None]
    column_div = lax.optimization_barrier(jnp.sum(divergence, axis=0)) / math.sqrt(divergence.shape[0])
    return jnp.stack([-absolute_vort * divergence, absolute_vort * vorticity - divergence * column_div[None]]).astype(jnp.bfloat16)

def reference(spectral, legendre, wavenumber):
    kept_degrees = jnp.arange(NN, dtype=jnp.int32)[None, :] <= (TRUNC - wavenumber)[:, None]
    masked_spec = jnp.where(kept_degrees, spectral, jnp.zeros_like(spectral))
    legendre_f32 = legendre.astype(jnp.float32)
    fourier = jnp.einsum('flrsn,sjn->flrsj', masked_spec.astype(jnp.float32), legendre_f32).astype(jnp.bfloat16)
    band_index = jnp.arange(N_LEV, dtype=jnp.int32)

    def one_set(set_index):
        latitude = set_index * LS + jnp.arange(LS, dtype=jnp.int32)
        synth_table, analysis_table, planetary = circle_tables(latitude, band_index, wavenumber, NLAT, N_LEV, BC, MW)
        block = lax.dynamic_slice_in_dim(fourier, set_index * LS, LS, 4).astype(jnp.float32)
        grid_values = jnp.einsum('flrsq,qprs->flqp', block, synth_table.astype(jnp.float32))
        tendency = tendencies(grid_values, planetary)
        return jnp.einsum('flqp,qprs->flrsq', tendency.astype(jnp.float32), analysis_table.astype(jnp.float32)).astype(jnp.bfloat16)
    set_blocks = lax.map(one_set, jnp.arange(N_WAVE, dtype=jnp.int32))
    tend_fourier = jnp.moveaxis(set_blocks, 0, 4).reshape(2, LEVELS, 2, MW, NLAT)
    analysed = jnp.einsum('flrsj,sjn->flrsn', tend_fourier.astype(jnp.float32), legendre_f32)
    return jnp.where(kept_degrees, analysed, jnp.zeros_like(analysed)).astype(jnp.bfloat16)
```

```python
import math

import jax
import jax.numpy as jnp
from jax import lax
from jax.experimental import pallas as pl
from jax.experimental.pallas import tpu as pltpu
from jax.sharding import PartitionSpec as P

LATS = 2560
DEG = 1280
SETS = 32
SPAN = 80
LANES = 128
ROWS = (16, 24, 32, 40, 48)
F32 = jnp.float32
BF16 = jnp.bfloat16


def cos_turns(f):
    r = f - jnp.round(f)
    y = 0.25 - jnp.abs(r)
    z = y * y
    tau = 2.0 * math.pi
    coef = [(-1.0) ** k * tau ** (2 * k + 1) / math.factorial(2 * k + 1) for k in range(6)]
    acc = jnp.full_like(z, coef[5])
    for c in coef[4::-1]:
        acc = acc * z + c
    return acc * y


def turns(product, inv, length):
    q = jnp.round(product * inv)
    return (product - q * length) * inv


def fetch_copies(leg, table, sems):
    copies = []
    for w in range(SETS):
        for q in range(5):
            copies.append(
                pltpu.make_async_copy(
                    leg.at[q, w], table.at[w, 8 * q : 8 * q + 8], sems.at[w * 10 + q]
                )
            )
            copies.append(
                pltpu.make_async_copy(
                    leg.at[5 + q, SETS - 1 - w],
                    table.at[w, 40 + 8 * q : 48 + 8 * q],
                    sems.at[w * 10 + 5 + q],
                )
            )
    return copies


def forward_kernel(spec, leg, out, table, sems):
    copies = fetch_copies(leg, table, sems)
    for c in copies:
        c.start()
    rows = spec[...]
    for w in range(SETS):
        for c in copies[10 * w : 10 * w + 10]:
            c.wait()
        got = lax.dot_general(
            rows, table[w], (((1,), (1,)), ((), ())), preferred_element_type=F32
        )
        out[w, :, 0:SPAN] = got.astype(BF16)
        out[w, :, SPAN:] = jnp.zeros((8, LANES - SPAN), BF16)


def inverse_kernel(coef, leg, out, table, sems):
    copies = fetch_copies(leg, table, sems)
    for c in copies:
        c.start()
    acc = jnp.zeros((8, DEG), F32)
    for w in range(SETS):
        for c in copies[10 * w : 10 * w + 10]:
            c.wait()
        acc += jnp.dot(coef[w, :, 0:SPAN], table[w], preferred_element_type=F32)
    out[...] = acc


def grid_kernel(wave_f, fin, out, wide, lines, sums):
    me = lax.axis_index("wave")
    wide[...] = fin[...].astype(F32).reshape(SETS * 8, LANES)
    scale = 1.0 / math.sqrt(SETS)
    for k in range(3):
        re = wide[pl.ds(2 * k, SETS, stride=8), :] * scale
        im = wide[pl.ds(2 * k + 1, SETS, stride=8), :] * scale
        lines[k] = jnp.concatenate([re, im, -im, re], axis=0).T
    m_row = wave_f[...]
    m_lane = jnp.concatenate([m_row] * 4, axis=1)
    m_sub = jnp.broadcast_to(m_lane, (LANES, LANES)).T
    t_lane = lax.broadcasted_iota(jnp.int32, (64, LANES), 1).astype(F32)
    fine_base = m_sub[0:64] * t_lane
    fine_shift = jnp.where(
        lax.broadcasted_iota(jnp.int32, (64, LANES), 0) < SETS, 0.0, 0.25
    )

    def latitude(q, r, rows):
        n = 8 * q + r
        j = 256 * q + 8 * me + r
        length = jnp.full((8, LANES), 20 + 4 * j, jnp.int32).astype(F32)
        inv = 1.0 / length
        turn = (jnp.full((8, LANES), j, jnp.int32).astype(F32) + 0.5) / 5120.0
        planet = 2.0 * cos_turns(turn)[0:1]
        weight = (cos_turns(turn - 0.25) * lax.rsqrt(length))[0:1]
        length, inv = length[0:1], inv[0:1]
        fine = cos_turns(turns(fine_base, inv, length) + fine_shift).astype(BF16)
        fine = jnp.concatenate([fine, fine], axis=0)
        a_sub = lax.broadcasted_iota(jnp.int32, (rows, LANES), 0)
        lane = lax.broadcasted_iota(jnp.int32, (rows, LANES), 1)
        coarse_shift = jnp.where(lane < 64, 0.0, 0.25)
        coarse = cos_turns(
            turns((a_sub * LANES).astype(F32) * m_lane, inv, length) - coarse_shift
        )
        parts = []
        for k in range(3):
            for at in (n, 79 - n):
                parts.append(lines[k, pl.ds(at, 1), :] * coarse)
        left = jnp.concatenate(parts, axis=0).astype(BF16)
        grid = jnp.dot(left, fine, preferred_element_type=F32)
        inside = (a_sub * LANES + lane) < (20 + 4 * j)
        tend = []
        for h, sign in ((0, 1.0), (1, -1.0)):
            vort = grid[h * rows : (h + 1) * rows]
            div = grid[(2 + h) * rows : (3 + h) * rows]
            col = grid[(4 + h) * rows : (5 + h) * rows]
            total = vort + sign * planet
            tend.append((jnp.where(inside, -total * div, 0.0), jnp.where(inside, total * vort - div * col, 0.0)))
        right = jnp.concatenate([tend[0][0], tend[1][0], tend[0][1], tend[1][1]], axis=0)
        back = lax.dot_general(
            right.astype(BF16), fine, (((1,), (1,)), ((), ())), preferred_element_type=F32
        )
        for i in range(4):
            at = n if i % 2 == 0 else 79 - n
            line = jnp.sum(back[i * rows : (i + 1) * rows] * coarse, axis=0, keepdims=True)
            sums[i // 2, pl.ds(at, 1), :] = line * weight

    sums[...] = jnp.zeros_like(sums)
    for q in range(5):

        @pl.loop(0, 4)
        def _(step, q=q):
            for u in range(2):
                latitude(q, 2 * step + u, ROWS[q])

    for k in range(2):
        cols = sums[k].T
        wide[pl.ds(2 * k, SETS, stride=8), :] = cols[0:32] + cols[96:128]
        wide[pl.ds(2 * k + 1, SETS, stride=8), :] = cols[32:64] - cols[64:96]
        wide[pl.ds(2 * k + 4, SETS, stride=8), :] = jnp.zeros((SETS, LANES), F32)
        wide[pl.ds(2 * k + 5, SETS, stride=8), :] = jnp.zeros((SETS, LANES), F32)
    out[...] = wide[...].reshape(SETS, 8, LANES).astype(BF16)


def vmem():
    return pl.BlockSpec(memory_space=pltpu.VMEM)


def body(spectral, legendre, wavenumber):
    own = lax.dynamic_slice_in_dim(wavenumber, lax.axis_index("wave"), 1, 0)
    kept = jnp.arange(DEG, dtype=jnp.int32)[None, :] <= (DEG - 1 - own)[:, None]
    spec = spectral.reshape(4, DEG)
    spec = jnp.where(kept, spec, jnp.zeros_like(spec))
    column = lax.psum(spec[2:4].astype(F32), "lev") / math.sqrt(SETS)
    rows = jnp.concatenate([spec, column.astype(BF16), jnp.zeros((2, DEG), BF16)], axis=0)
    leg = legendre.reshape(10, SETS, 8, DEG)
    table = [pltpu.VMEM((SETS, SPAN, DEG), BF16), pltpu.SemaphoreType.DMA((SETS * 10,))]
    sent = pl.pallas_call(
        forward_kernel,
        out_shape=jax.ShapeDtypeStruct((SETS, 8, LANES), BF16),
        in_specs=[vmem(), pl.BlockSpec(memory_space=pl.ANY)],
        out_specs=vmem(),
        scratch_shapes=table,
    )(rows, leg)
    got = lax.all_to_all(sent, "wave", split_axis=0, concat_axis=0, tiled=True)
    tend = pl.pallas_call(
        grid_kernel,
        out_shape=jax.ShapeDtypeStruct((SETS, 8, LANES), BF16),
        in_specs=[vmem(), vmem()],
        out_specs=vmem(),
        scratch_shapes=[
            pltpu.VMEM((SETS * 8, LANES), F32),
            pltpu.VMEM((3, LANES, LANES), F32),
            pltpu.VMEM((2, LANES, LANES), F32),
        ],
    )(wavenumber.astype(F32)[None, :], got)
    back = lax.all_to_all(tend, "wave", split_axis=0, concat_axis=0, tiled=True)
    analysed = pl.pallas_call(
        inverse_kernel,
        out_shape=jax.ShapeDtypeStruct((8, DEG), F32),
        in_specs=[vmem(), pl.BlockSpec(memory_space=pl.ANY)],
        out_specs=vmem(),
        scratch_shapes=table,
    )(back, leg)[0:4]
    shown = jnp.where(kept, analysed, jnp.zeros_like(analysed)).astype(BF16)
    return shown.reshape(2, 1, 2, 1, DEG)


def solution(mesh):
    in_specs = (P(None, "lev", None, "wave", None), P("wave", None, None), P())
    out_specs = P(None, "lev", None, "wave", None)
    return jax.shard_map(body, mesh=mesh, in_specs=in_specs, out_specs=out_specs, check_vma=False)
```

```python
import functools
import math

import jax
import jax.numpy as jnp
from jax import lax
from jax.experimental import pallas as pl
from jax.experimental.pallas import tpu as pltpu
from jax.sharding import PartitionSpec as P

LATS = 2560
DEG = 1280
SETS = 32
LEVELS = 32
LANES = 128
HOP = 2
NODES = LEVELS // HOP
RIGHT = NODES // 2
LEFT = NODES - 1 - RIGHT
ROWS = (16, 24, 32, 40, 48)
F32 = jnp.float32
BF16 = jnp.bfloat16
MESH = pl.DeviceIdType.MESH


def cos_turns(f):
    r = f - jnp.round(f)
    y = 0.25 - jnp.abs(r)
    z = y * y
    tau = 2.0 * math.pi
    coef = [(-1.0) ** k * tau ** (2 * k + 1) / math.factorial(2 * k + 1) for k in range(6)]
    acc = jnp.full_like(z, coef[5])
    for c in coef[4::-1]:
        acc = acc * z + c
    return acc * y


def turns(product, inv, length):
    q = jnp.round(product * inv)
    return (product - q * length) * inv


def kernel(spec, waves, leg, out, *scratch):
    (table, table_sem, xt, zs, sends, gets, wide, lines, sums, fine_s, pair_s, deg_s) = scratch[:12]
    coarse_s = scratch[12:17]
    grid_s = scratch[17:22]
    (own_s, near_s, node_s, right_s, left_s, near_sem, right_sem, left_sem, plane_sem) = scratch[22:]
    me = lax.axis_index("wave")
    lev = lax.axis_index("lev")

    loads = [
        pltpu.make_async_copy(
            leg.at[pl.ds(256 * q, 256)], table.at[pl.ds(256 * q, 256)], table_sem.at[q]
        )
        for q in range(10)
    ]
    for c in loads:
        c.start()

    barrier = pltpu.get_barrier_semaphore()

    def greet(d, _):
        pl.semaphore_signal(
            barrier, inc=1, device_id=(lax.rem(me + d, SETS), lev), device_id_type=MESH
        )
        return 0

    z_peers = sorted({1, LEVELS - 1, HOP, LEVELS - HOP})
    for d in z_peers:
        pl.semaphore_signal(
            barrier, inc=1, device_id=(me, lax.rem(lev + d, LEVELS)), device_id_type=MESH
        )
    lax.fori_loop(1, SETS, greet, 0)

    m_lane = jnp.concatenate([waves[...].astype(F32)] * 4, axis=1)
    m_sub = jnp.broadcast_to(m_lane, (LANES, LANES)).T
    lane8 = lax.broadcasted_iota(jnp.int32, (8, LANES), 1)
    own_m = jnp.sum(jnp.where(lane8[0:1, 0:SETS] == me, m_lane[:, 0:SETS], 0.0), axis=1, keepdims=True)
    degree = lax.broadcasted_iota(jnp.int32, (4, DEG), 1).astype(F32)
    kept = degree <= (DEG - 1.0) - own_m
    rows = jnp.concatenate([spec[0].astype(F32), spec[1].astype(F32)], axis=0)
    rows = jnp.where(kept, rows, 0.0)
    own_s[...] = rows[2:4].astype(BF16)
    group_of = lane8 // 8
    group_masks = [group_of == g for g in range(16)]

    def set_right(x):
        block = jnp.concatenate([x, jnp.zeros((8 - x.shape[0], DEG), F32)], axis=0)
        block = jnp.concatenate([block] * 16, axis=0)
        for k in range(10):
            xt[LANES * k : LANES * (k + 1), :] = block[:, LANES * k : LANES * (k + 1)].T.astype(BF16)

    def product(q):
        got = jnp.dot(table[256 * q : 256 * q + 256, :], xt[...], preferred_element_type=F32)
        for b in range(2):
            acc = jnp.zeros((8, LANES), F32)
            for g in range(16):
                w = 16 * b + g
                w = w if q < 5 else SETS - 1 - w
                acc = jnp.where(group_masks[g], got[8 * w : 8 * w + 8], acc)
            zs[b, 8 * q : 8 * q + 8, :] = acc

    def post(stage):
        for b in range(2):
            sends[stage, 16 * b : 16 * b + 16] = zs[b].T.reshape(16, 8, LANES).astype(BF16)

    def plane_copy(stage, d):
        to = lax.rem(me + d, SETS)
        return pltpu.make_async_remote_copy(
            src_ref=sends.at[stage, to],
            dst_ref=gets.at[stage, me],
            send_sem=plane_sem.at[stage, 0, d],
            recv_sem=plane_sem.at[stage, 1, d],
            device_id=(to, lev),
            device_id_type=MESH,
        )

    def plane_start(stage):
        def one(d, _):
            plane_copy(stage, d).start()
            return 0

        lax.fori_loop(1, SETS, one, 0)
        gets[stage, me] = sends[stage, me]

    def plane_wait(stage):
        def one(d, _):
            origin = lax.rem(me - d + SETS, SETS)
            pltpu.make_async_remote_copy(
                src_ref=sends.at[stage, lax.rem(me + d, SETS)],
                dst_ref=gets.at[stage, origin],
                send_sem=plane_sem.at[stage, 0, d],
                recv_sem=plane_sem.at[stage, 1, d],
                device_id=(origin, lev),
                device_id_type=MESH,
            ).wait()
            return 0

        lax.fori_loop(1, SETS, one, 0)

    def z_copy(src, dst, sems, i, shift):
        return pltpu.make_async_remote_copy(
            src_ref=src,
            dst_ref=dst,
            send_sem=sems.at[0, i],
            recv_sem=sems.at[1, i],
            device_id=(me, lax.rem(lev + shift, LEVELS)),
            device_id_type=MESH,
        )

    near = z_copy(own_s, near_s, near_sem, 0, LEVELS - 1)
    rights = [
        z_copy(node_s if s == 0 else right_s.at[s - 1], right_s.at[s], right_sem, s, HOP)
        for s in range(RIGHT)
    ]
    lefts = [
        z_copy(node_s if s == 0 else left_s.at[s - 1], left_s.at[s], left_sem, s, LEVELS - HOP)
        for s in range(LEFT)
    ]

    def ring(s):
        if s < RIGHT:
            rights[s].wait_recv()
            if s + 1 < RIGHT:
                rights[s + 1].start()
        if s < LEFT:
            lefts[s].wait_recv()
            if s + 1 < LEFT:
                lefts[s + 1].start()

    t_lane = lax.broadcasted_iota(jnp.int32, (64, LANES), 1).astype(F32)

    def tables(q):
        a_sub = lax.broadcasted_iota(jnp.int32, (ROWS[q], LANES), 0)
        lane = lax.broadcasted_iota(jnp.int32, (ROWS[q], LANES), 1)
        coarse_base = (a_sub * LANES).astype(F32) * m_lane
        coarse_shift = jnp.where(lane < 64, 0.0, 0.25)
        fine_base = m_sub[0:64] * t_lane
        fine_shift = jnp.where(lax.broadcasted_iota(jnp.int32, (64, LANES), 0) < SETS, 0.0, 0.25)

        def one(r, _):
            n = 8 * q + r
            j = 256 * q + 8 * me + r
            length = jnp.full((8, LANES), 20 + 4 * j, jnp.int32).astype(F32)
            inv = 1.0 / length
            turn = (jnp.full((8, LANES), j, jnp.int32).astype(F32) + 0.5) / 5120.0
            planet = 2.0 * cos_turns(turn)
            weight = cos_turns(turn - 0.25) * lax.rsqrt(length)
            pair_s[n, 0] = planet
            pair_s[n, 1] = weight
            length, inv = length[0:1], inv[0:1]
            fine = cos_turns(turns(fine_base, inv, length) + fine_shift).astype(BF16)
            fine_s[n, 0:64] = fine
            fine_s[n, 64:128] = fine
            coarse_s[q][r] = cos_turns(turns(coarse_base, inv, length) - coarse_shift)
            return 0

        lax.fori_loop(0, 8, one, 0, unroll=2)

    scale = 1.0 / math.sqrt(LEVELS)

    def take_lines(stage, count, base):
        wide[...] = gets[stage].astype(F32).reshape(SETS * 8, LANES)
        for k in range(count):
            re = wide[pl.ds(2 * k, SETS, stride=8), :] * scale
            im = wide[pl.ds(2 * k + 1, SETS, stride=8), :] * scale
            lines[base + k] = jnp.concatenate([re, im, -im, re], axis=0).T

    def synth(q):
        def one(r, _):
            n = 8 * q + r
            coarse = coarse_s[q][r]
            parts = [
                lines[k, pl.ds(at, 1), :] * coarse for k in range(2) for at in (n, 79 - n)
            ]
            left = jnp.concatenate(parts, axis=0).astype(BF16)
            grid_s[q][r] = jnp.dot(left, fine_s[n], preferred_element_type=F32)
            return 0

        lax.fori_loop(0, 8, one, 0, unroll=2)

    def finish(q):
        count = ROWS[q]
        a_sub = lax.broadcasted_iota(jnp.int32, (count, LANES), 0)
        lane = lax.broadcasted_iota(jnp.int32, (count, LANES), 1)
        point = a_sub * LANES + lane

        def one(r, _):
            n = 8 * q + r
            j = 256 * q + 8 * me + r
            coarse = coarse_s[q][r]
            fine = fine_s[n]
            planet = pair_s[n, 0, 0:1]
            weight = pair_s[n, 1, 0:1]
            left = jnp.concatenate(
                [lines[2, pl.ds(at, 1), :] * coarse for at in (n, 79 - n)], axis=0
            ).astype(BF16)
            col = jnp.dot(left, fine, preferred_element_type=F32)
            inside = point < (20 + 4 * j)
            first, second = [], []
            for h, sign in ((0, 1.0), (1, -1.0)):
                vort = grid_s[q][r, h * count : (h + 1) * count]
                div = grid_s[q][r, (2 + h) * count : (3 + h) * count]
                total = vort + sign * planet
                first.append(jnp.where(inside, -total * div, 0.0))
                second.append(
                    jnp.where(inside, total * vort - div * col[h * count : (h + 1) * count], 0.0)
                )
            tend = jnp.concatenate(first + second, axis=0).astype(BF16)
            back = lax.dot_general(
                tend, fine, (((1,), (1,)), ((), ())), preferred_element_type=F32
            )
            for i in range(4):
                at = n if i % 2 == 0 else 79 - n
                line = jnp.sum(back[i * count : (i + 1) * count] * coarse, axis=0, keepdims=True)
                sums[i // 2, pl.ds(at, 1), :] = line * weight
            return 0

        lax.fori_loop(0, 8, one, 0, unroll=4)

    set_right(rows)
    zs[...] = jnp.zeros_like(zs)
    sums[...] = jnp.zeros_like(sums)
    pl.semaphore_wait(barrier, SETS - 1 + len(z_peers))
    near.start()
    for q in range(5):
        loads[q].wait()
        product(q)
    near.wait_recv()
    node_s[...] = (rows[2:4] + near_s[...].astype(F32)).astype(BF16)
    for q in range(5, 7):
        loads[q].wait()
        product(q)
    rights[0].start()
    lefts[0].start()
    for q in range(7, 10):
        loads[q].wait()
        product(q)
    post(0)
    ring(0)
    tables(0)
    plane_start(0)
    tables(1)
    ring(1)
    tables(2)
    tables(3)
    ring(2)
    tables(4)
    plane_wait(0)
    take_lines(0, 2, 0)
    ring(3)
    synth(0)
    synth(1)
    ring(4)
    synth(2)
    ring(5)
    synth(3)
    ring(6)
    synth(4)
    for s in range(7, max(RIGHT, LEFT)):
        ring(s)
    total = node_s[...].astype(F32)
    for s in range(RIGHT):
        total += right_s[s].astype(F32)
    for s in range(LEFT):
        total += left_s[s].astype(F32)
    set_right(total * scale)
    for q in range(10):
        product(q)
    post(1)
    near.wait_send()
    for c in rights + lefts:
        c.wait_send()
    plane_start(1)
    plane_wait(1)
    take_lines(1, 1, 2)
    for q in range(5):
        finish(q)
    for k in range(2):
        cols = sums[k].T
        wide[pl.ds(2 * k, SETS, stride=8), :] = cols[0:32] + cols[96:128]
        wide[pl.ds(2 * k + 1, SETS, stride=8), :] = cols[32:64] - cols[64:96]
        wide[pl.ds(2 * k + 4, SETS, stride=8), :] = jnp.zeros((SETS, LANES), F32)
        wide[pl.ds(2 * k + 5, SETS, stride=8), :] = jnp.zeros((SETS, LANES), F32)
    sends[2] = wide[...].reshape(SETS, 8, LANES).astype(BF16)
    plane_start(2)
    plane_wait(2)
    wide[...] = gets[2].astype(F32).reshape(SETS * 8, LANES)
    for q in range(10):
        for b in range(2):
            acc = jnp.zeros((8, LANES), F32)
            for g in range(16):
                w = 16 * b + g
                w = w if q < 5 else SETS - 1 - w
                piece = pltpu.roll(wide[8 * w : 8 * w + 8, :], (8 * g - 8 * q) % LANES, 1)
                acc = jnp.where(group_masks[g], piece, acc)
            deg_s[:, 256 * q + LANES * b : 256 * q + LANES * (b + 1)] = acc
    result = jnp.dot(deg_s[...].astype(BF16), table[...], preferred_element_type=F32)[0:4]
    result = jnp.where(kept, result, 0.0)
    out[0] = result[0:2].astype(BF16)
    out[1] = result[2:4].astype(BF16)


def body(spectral, legendre, wavenumber):
    anywhere = pl.BlockSpec(memory_space=pl.ANY)
    local = pl.BlockSpec(memory_space=pltpu.VMEM)
    dma = pltpu.SemaphoreType.DMA
    scratch = [
        pltpu.VMEM((LATS, DEG), BF16),
        dma((10,)),
        pltpu.VMEM((DEG, LANES), BF16),
        pltpu.VMEM((2, LANES, LANES), F32),
        pltpu.VMEM((3, SETS, 8, LANES), BF16),
        pltpu.VMEM((3, SETS, 8, LANES), BF16),
        pltpu.VMEM((SETS * 8, LANES), F32),
        pltpu.VMEM((3, LANES, LANES), F32),
        pltpu.VMEM((2, LANES, LANES), F32),
        pltpu.VMEM((40, LANES, LANES), BF16),
        pltpu.VMEM((40, 2, 8, LANES), F32),
        pltpu.VMEM((8, LATS), F32),
    ]
    scratch += [pltpu.VMEM((8, n, LANES), F32) for n in ROWS]
    scratch += [pltpu.VMEM((8, 4 * n, LANES), F32) for n in ROWS]
    scratch += [
        pltpu.VMEM((2, DEG), BF16),
        pltpu.VMEM((2, DEG), BF16),
        pltpu.VMEM((2, DEG), BF16),
        pltpu.VMEM((RIGHT, 2, DEG), BF16),
        pltpu.VMEM((LEFT, 2, DEG), BF16),
        dma((2, 1)),
        dma((2, RIGHT)),
        dma((2, LEFT)),
        dma((3, 2, SETS)),
    ]
    result = pl.pallas_call(
        kernel,
        out_shape=jax.ShapeDtypeStruct((2, 2, DEG), BF16),
        in_specs=[local, local, anywhere],
        out_specs=local,
        scratch_shapes=scratch,
        compiler_params=pltpu.CompilerParams(
            collective_id=0, has_side_effects=True, vmem_limit_bytes=48 * 1024 * 1024
        ),
    )(spectral.reshape(2, 2, DEG), wavenumber.reshape(1, SETS), legendre.reshape(LATS, DEG))
    return result.reshape(2, 1, 2, 1, DEG)


def solution(mesh):
    in_specs = (P(None, "lev", None, "wave", None), P("wave", None, None), P())
    out_specs = P(None, "lev", None, "wave", None)
    return jax.shard_map(body, mesh=mesh, in_specs=in_specs, out_specs=out_specs, check_vma=False)
```

```python
import functools
import math

import jax
import jax.numpy as jnp
from jax import lax
from jax.experimental import pallas as pl
from jax.experimental.pallas import tpu as pltpu
from jax.sharding import PartitionSpec as P

LATS = 2560
DEG = 1280
SETS = 32
LEVELS = 32
LANES = 128
HOP = 8
NODES = LEVELS // HOP
RIGHT = NODES // 2
NEAR = [o for o in range(1 - HOP // 2, HOP // 2 + 1) if o] if HOP > 1 else []
LEFT = NODES - 1 - RIGHT
FINISH = 4
ROWS = (16, 24, 32, 40, 48)
F32 = jnp.float32
BF16 = jnp.bfloat16
MESH = pl.DeviceIdType.MESH


def cos_turns(f):
    r = f - jnp.round(f)
    y = 0.25 - jnp.abs(r)
    z = y * y
    tau = 2.0 * math.pi
    coef = [(-1.0) ** k * tau ** (2 * k + 1) / math.factorial(2 * k + 1) for k in range(6)]
    acc = jnp.full_like(z, coef[5])
    for c in coef[4::-1]:
        acc = acc * z + c
    return acc * y


def turns(product, inv, length):
    q = jnp.round(product * inv)
    return (product - q * length) * inv


def kernel(spec_in, waves_in, leg, out, *scratch):
    (spec, waves, in_sem, table, table_sem, sends, gets, wide, lines, sums, fine_s, pair_s, nat_s) = scratch[:13]
    coarse_s = scratch[13:18]
    grid_s = scratch[18:23]
    (own_s, near_s, node_s, total_s, right_s, left_s, near_sem, right_sem, left_sem, plane_sem) = scratch[23:]
    me = lax.axis_index("wave")
    lev = lax.axis_index("lev")

    inputs = [
        pltpu.make_async_copy(spec_in, spec, in_sem.at[0]),
        pltpu.make_async_copy(waves_in, waves, in_sem.at[1]),
    ]
    for c in inputs:
        c.start()
    loads = [
        pltpu.make_async_copy(
            leg.at[pl.ds(256 * q, 256)], table.at[pl.ds(256 * q, 256)], table_sem.at[q]
        )
        for q in range(10)
    ]
    for c in loads:
        c.start()

    barrier = pltpu.get_barrier_semaphore()

    def greet(d, _):
        pl.semaphore_signal(
            barrier, inc=1, device_id=(lax.rem(me + d, SETS), lev), device_id_type=MESH
        )
        return 0

    z_peers = sorted({o % LEVELS for n in NEAR + [HOP] for o in (n, -n)})
    for d in z_peers:
        pl.semaphore_signal(
            barrier, inc=1, device_id=(me, lax.rem(lev + d, LEVELS)), device_id_type=MESH
        )
    lax.fori_loop(1, SETS, greet, 0)

    for c in inputs:
        c.wait()
    m_lane = jnp.concatenate([waves[...].astype(F32)] * 4, axis=1)
    m_sub = jnp.broadcast_to(m_lane, (LANES, LANES)).T
    lane8 = lax.broadcasted_iota(jnp.int32, (8, LANES), 1)
    own_m = jnp.sum(jnp.where(lane8[0:1, 0:SETS] == me, m_lane[:, 0:SETS], 0.0), axis=1, keepdims=True)
    degree = lax.broadcasted_iota(jnp.int32, (4, DEG), 1).astype(F32)
    kept = degree <= (DEG - 1.0) - own_m
    rows = jnp.concatenate([spec[0].astype(F32), spec[1].astype(F32)], axis=0)
    rows = jnp.where(kept, rows, 0.0)
    own_s[...] = rows[2:4].astype(BF16)
    group_of = lane8 // 8
    group_masks = [group_of == g for g in range(16)]

    def eight(x):
        pad = jnp.zeros((8 - x.shape[0], DEG), F32)
        return jnp.concatenate([x, pad], axis=0).astype(BF16)

    def product(left, q):
        nat_s[:, 256 * q : 256 * q + 256] = lax.dot_general(
            left,
            table[256 * q : 256 * q + 256, :],
            (((1,), (1,)), ((), ())),
            preferred_element_type=F32,
        )

    def post(stage):
        for w in range(SETS):
            acc = None
            for q in range(10):
                chunk = w if q < 5 else SETS - 1 - w
                at = 256 * q + LANES * (chunk // 16)
                shift = (8 * q - 8 * (chunk % 16)) % LANES
                piece = nat_s[:, at : at + LANES]
                piece = pltpu.roll(piece, shift, 1) if shift else piece
                acc = piece if acc is None else jnp.where(group_masks[q], piece, acc)
            sends[stage, w] = acc.astype(BF16)

    def plane_copy(stage, d):
        to = lax.rem(me + d, SETS)
        return pltpu.make_async_remote_copy(
            src_ref=sends.at[stage, to],
            dst_ref=gets.at[stage, me],
            send_sem=plane_sem.at[stage, 0, d],
            recv_sem=plane_sem.at[stage, 1, d],
            device_id=(to, lev),
            device_id_type=MESH,
        )

    def plane_start(stage):
        def one(d, _):
            plane_copy(stage, d).start()
            return 0

        lax.fori_loop(1, SETS, one, 0, unroll=True)
        gets[stage, me] = sends[stage, me]

    def plane_wait(stage):
        def one(d, _):
            origin = lax.rem(me - d + SETS, SETS)
            pltpu.make_async_remote_copy(
                src_ref=sends.at[stage, lax.rem(me + d, SETS)],
                dst_ref=gets.at[stage, origin],
                send_sem=plane_sem.at[stage, 0, d],
                recv_sem=plane_sem.at[stage, 1, d],
                device_id=(origin, lev),
                device_id_type=MESH,
            ).wait()
            return 0

        lax.fori_loop(1, SETS, one, 0, unroll=True)

    def z_copy(src, dst, sems, i, shift):
        return pltpu.make_async_remote_copy(
            src_ref=src,
            dst_ref=dst,
            send_sem=sems.at[0, i],
            recv_sem=sems.at[1, i],
            device_id=(me, lax.rem(lev + shift, LEVELS)),
            device_id_type=MESH,
        )

    nears = [
        z_copy(own_s, near_s.at[i], near_sem, i, (-o) % LEVELS) for i, o in enumerate(NEAR)
    ]
    rights = [
        z_copy(node_s if s == 0 else right_s.at[s - 1], right_s.at[s], right_sem, s, HOP)
        for s in range(RIGHT)
    ]
    lefts = [
        z_copy(node_s if s == 0 else left_s.at[s - 1], left_s.at[s], left_sem, s, LEVELS - HOP)
        for s in range(LEFT)
    ]

    def ring(s):
        if s < RIGHT:
            rights[s].wait_recv()
            if s + 1 < RIGHT:
                rights[s + 1].start()
            total_s[...] += right_s[s].astype(F32)
        if s < LEFT:
            lefts[s].wait_recv()
            if s + 1 < LEFT:
                lefts[s + 1].start()
            total_s[...] += left_s[s].astype(F32)

    t_lane = lax.broadcasted_iota(jnp.int32, (64, LANES), 1).astype(F32)

    def tables(q):
        a_sub = lax.broadcasted_iota(jnp.int32, (ROWS[q], LANES), 0)
        lane = lax.broadcasted_iota(jnp.int32, (ROWS[q], LANES), 1)
        coarse_base = (a_sub * LANES).astype(F32) * m_lane
        coarse_shift = jnp.where(lane < 64, 0.0, 0.25)
        fine_base = m_sub[0:64] * t_lane
        fine_shift = jnp.where(lax.broadcasted_iota(jnp.int32, (64, LANES), 0) < SETS, 0.0, 0.25)

        def one(r, _):
            n = 8 * q + r
            j = 256 * q + 8 * me + r
            length = jnp.full((8, LANES), 20 + 4 * j, jnp.int32).astype(F32)
            inv = 1.0 / length
            turn = (jnp.full((8, LANES), j, jnp.int32).astype(F32) + 0.5) / 5120.0
            planet = 2.0 * cos_turns(turn)
            weight = cos_turns(turn - 0.25) * lax.rsqrt(length)
            pair_s[n, 0] = planet
            pair_s[n, 1] = weight
            length, inv = length[0:1], inv[0:1]
            fine = cos_turns(turns(fine_base, inv, length) + fine_shift).astype(BF16)
            fine_s[n, 0:64] = fine
            fine_s[n, 64:128] = fine
            coarse_s[q][r] = cos_turns(turns(coarse_base, inv, length) - coarse_shift)
            return 0

        lax.fori_loop(0, 8, one, 0, unroll=2)

    scale = 1.0 / math.sqrt(LEVELS)

    def take_lines(stage, count, base):
        wide[...] = gets[stage].astype(F32).reshape(SETS * 8, LANES)
        for k in range(count):
            re = wide[pl.ds(2 * k, SETS, stride=8), :] * scale
            im = wide[pl.ds(2 * k + 1, SETS, stride=8), :] * scale
            lines[base + k] = jnp.concatenate([re, im, -im, re], axis=0).T

    def shown(x, inside):
        count = x.shape[0]
        tail = jnp.where(inside, x[count - 16 :], 0.0)
        return tail if count == 16 else jnp.concatenate([x[: count - 16], tail], axis=0)

    def analyse(field, parts, n, coarse, fine, weight):
        count = coarse.shape[0]
        tend = jnp.concatenate(parts, axis=0).astype(BF16)
        back = lax.dot_general(tend, fine, (((1,), (1,)), ((), ())), preferred_element_type=F32)
        for h, at in enumerate((n, 79 - n)):
            line = jnp.sum(back[h * count : (h + 1) * count] * coarse, axis=0, keepdims=True)
            sums[field, pl.ds(at, 1), :] = line * weight

    def synth(q):
        count = ROWS[q]
        a_sub = lax.broadcasted_iota(jnp.int32, (16, LANES), 0) + (count - 16)
        point = a_sub * LANES + lax.broadcasted_iota(jnp.int32, (16, LANES), 1)

        def one(r, _):
            n = 8 * q + r
            j = 256 * q + 8 * me + r
            coarse = coarse_s[q][r]
            fine = fine_s[n]
            planet = pair_s[n, 0, 0:1]
            parts = [
                lines[k, pl.ds(at, 1), :] * coarse for k in range(2) for at in (n, 79 - n)
            ]
            left = jnp.concatenate(parts, axis=0).astype(BF16)
            grid = jnp.dot(left, fine, preferred_element_type=F32)
            inside = point < (20 + 4 * j)
            first = []
            for h, sign in ((0, 1.0), (1, -1.0)):
                vort = grid[h * count : (h + 1) * count]
                div = shown(grid[(2 + h) * count : (3 + h) * count], inside)
                total = vort + sign * planet
                first.append(total * div)
                grid_s[q][r, h * count : (h + 1) * count] = shown(total * vort, inside)
                grid_s[q][r, (2 + h) * count : (3 + h) * count] = div
            analyse(0, first, n, coarse, fine, -pair_s[n, 1, 0:1])
            return 0

        lax.fori_loop(0, 8, one, 0, unroll=2)

    def finish(q):
        count = ROWS[q]

        def one(r, _):
            n = 8 * q + r
            coarse = coarse_s[q][r]
            fine = fine_s[n]
            left = jnp.concatenate(
                [lines[2, pl.ds(at, 1), :] * coarse for at in (n, 79 - n)], axis=0
            ).astype(BF16)
            col = jnp.dot(left, fine, preferred_element_type=F32)
            second = grid_s[q][r, 0 : 2 * count] - grid_s[q][r, 2 * count : 4 * count] * col
            analyse(1, [second], n, coarse, fine, pair_s[n, 1, 0:1])
            return 0

        lax.fori_loop(0, 8, one, 0, unroll=FINISH)

    own = eight(rows)
    sums[...] = jnp.zeros_like(sums)
    pl.semaphore_wait(barrier, SETS - 1 + len(z_peers))
    for c in nears:
        c.start()

    def products(low, high):
        for q in range(low, high):
            loads[q].wait()
            product(own, q)

    def launch():
        node = rows[2:4]
        for i, c in enumerate(nears):
            c.wait_recv()
            node += near_s[i].astype(F32)
        node_s[...] = node.astype(BF16)
        total_s[...] = node_s[...].astype(F32)
        rights[0].start()
        lefts[0].start()

    def collect():
        plane_wait(0)
        take_lines(0, 2, 0)

    def send_own():
        plane_start(0)
        tables(0)

    work = [
        lambda: products(5, 8),
        lambda: (products(8, 10), post(0)),
        send_own,
        lambda: tables(1),
        lambda: tables(2),
        lambda: tables(3),
        lambda: tables(4),
        collect,
        lambda: synth(0),
        lambda: synth(1),
        lambda: synth(2),
        lambda: synth(3),
        lambda: synth(4),
    ]
    products(0, 5)
    launch()
    done = 0
    for i, item in enumerate(work):
        item()
        while done < (i + 1) * RIGHT // (len(work) + 1):
            ring(done)
            done += 1
    for s in range(done, RIGHT):
        ring(s)
    total = total_s[...]
    column = eight(total * scale)
    for q in range(10):
        product(column, q)
    post(1)
    for c in nears + rights + lefts:
        c.wait_send()
    plane_start(1)
    plane_wait(1)
    take_lines(1, 1, 2)
    for q in range(5):
        finish(q)
    for k in range(2):
        cols = sums[k].T
        wide[pl.ds(2 * k, SETS, stride=8), :] = cols[0:32] + cols[96:128]
        wide[pl.ds(2 * k + 1, SETS, stride=8), :] = cols[32:64] - cols[64:96]
        wide[pl.ds(2 * k + 4, SETS, stride=8), :] = jnp.zeros((SETS, LANES), F32)
        wide[pl.ds(2 * k + 5, SETS, stride=8), :] = jnp.zeros((SETS, LANES), F32)
    sends[2] = wide[...].reshape(SETS, 8, LANES).astype(BF16)
    plane_start(2)
    plane_wait(2)
    wide[...] = gets[2].astype(F32).reshape(SETS * 8, LANES)
    result = jnp.zeros((8, DEG), F32)
    for q in range(10):
        halves = []
        for b in range(2):
            acc = None
            for g in range(16):
                w = 16 * b + g
                w = w if q < 5 else SETS - 1 - w
                shift = (8 * g - 8 * q) % LANES
                piece = wide[8 * w : 8 * w + 8, :]
                piece = pltpu.roll(piece, shift, 1) if shift else piece
                acc = piece if acc is None else jnp.where(group_masks[g], piece, acc)
            halves.append(acc)
        left = jnp.concatenate(halves, axis=1).astype(BF16)
        result += jnp.dot(
            left, table[256 * q : 256 * q + 256, :], preferred_element_type=F32
        )
    result = result[0:4]
    result = jnp.where(kept, result, 0.0)
    out[0] = result[0:2].astype(BF16)
    out[1] = result[2:4].astype(BF16)


def body(spectral, legendre, wavenumber):
    anywhere = pl.BlockSpec(memory_space=pl.ANY)
    local = pl.BlockSpec(memory_space=pltpu.VMEM)
    dma = pltpu.SemaphoreType.DMA
    scratch = [
        pltpu.VMEM((2, 2, DEG), BF16),
        pltpu.VMEM((1, SETS), jnp.int32),
        dma((2,)),
        pltpu.VMEM((LATS, DEG), BF16),
        dma((10,)),
        pltpu.VMEM((3, SETS, 8, LANES), BF16),
        pltpu.VMEM((3, SETS, 8, LANES), BF16),
        pltpu.VMEM((SETS * 8, LANES), F32),
        pltpu.VMEM((3, LANES, LANES), F32),
        pltpu.VMEM((2, LANES, LANES), F32),
        pltpu.VMEM((40, LANES, LANES), BF16),
        pltpu.VMEM((40, 2, 8, LANES), F32),
        pltpu.VMEM((8, LATS), F32),
    ]
    scratch += [pltpu.VMEM((8, n, LANES), F32) for n in ROWS]
    scratch += [pltpu.VMEM((8, 4 * n, LANES), F32) for n in ROWS]
    scratch += [
        pltpu.VMEM((2, DEG), BF16),
        pltpu.VMEM((max(len(NEAR), 1), 2, DEG), BF16),
        pltpu.VMEM((2, DEG), BF16),
        pltpu.VMEM((2, DEG), F32),
        pltpu.VMEM((RIGHT, 2, DEG), BF16),
        pltpu.VMEM((LEFT, 2, DEG), BF16),
        dma((2, max(len(NEAR), 1))),
        dma((2, RIGHT)),
        dma((2, LEFT)),
        dma((3, 2, SETS)),
    ]
    result = pl.pallas_call(
        kernel,
        out_shape=jax.ShapeDtypeStruct((2, 2, DEG), BF16),
        in_specs=[anywhere, anywhere, anywhere],
        out_specs=local,
        scratch_shapes=scratch,
        compiler_params=pltpu.CompilerParams(
            collective_id=0, has_side_effects=True, vmem_limit_bytes=62_000_000
        ),
    )(spectral.reshape(2, 2, DEG), wavenumber.reshape(1, SETS), legendre.reshape(LATS, DEG))
    return result.reshape(2, 1, 2, 1, DEG)


def solution(mesh):
    in_specs = (P(None, "lev", None, "wave", None), P("wave", None, None), P())
    out_specs = P(None, "lev", None, "wave", None)
    return jax.shard_map(body, mesh=mesh, in_specs=in_specs, out_specs=out_specs, check_vma=False)
```

```python
import functools
import math

import jax
import jax.numpy as jnp
from jax import lax
from jax.experimental import pallas as pl
from jax.experimental.pallas import tpu as pltpu
from jax.sharding import PartitionSpec as P

LATS = 2560
DEG = 1280
SETS = 32
LEVELS = 32
LANES = 128
REACH = 5
SPAN = 2 * REACH + 1
NEAR = [o * side for o in range(REACH, 0, -1) for side in (1, -1)]
FINISH = 4
ROWS = (16, 24, 32, 40, 48)
F32 = jnp.float32
BF16 = jnp.bfloat16
MESH = pl.DeviceIdType.MESH


def cos_turns(f):
    r = f - jnp.round(f)
    y = 0.25 - jnp.abs(r)
    z = y * y
    tau = 2.0 * math.pi
    coef = [(-1.0) ** k * tau ** (2 * k + 1) / math.factorial(2 * k + 1) for k in range(6)]
    acc = jnp.full_like(z, coef[5])
    for c in coef[4::-1]:
        acc = acc * z + c
    return acc * y


def turns(product, inv, length):
    q = jnp.round(product * inv)
    return (product - q * length) * inv


def kernel(spec_in, waves_in, leg, out, *scratch):
    (spec, waves, in_sem, table, table_sem, sends, gets, wide, lines, sums, fine_s, pair_s, nat_s) = scratch[:13]
    coarse_s = scratch[13:18]
    grid_s = scratch[18:23]
    (own_s, near_s, node_s, far_s, near_sem, far_sem, plane_sem) = scratch[23:]
    me = lax.axis_index("wave")
    lev = lax.axis_index("lev")

    inputs = [
        pltpu.make_async_copy(spec_in, spec, in_sem.at[0]),
        pltpu.make_async_copy(waves_in, waves, in_sem.at[1]),
    ]
    for c in inputs:
        c.start()
    loads = [
        pltpu.make_async_copy(
            leg.at[pl.ds(256 * q, 256)], table.at[pl.ds(256 * q, 256)], table_sem.at[q]
        )
        for q in range(10)
    ]
    for c in loads:
        c.start()

    barrier = pltpu.get_barrier_semaphore()

    def greet(d, _):
        pl.semaphore_signal(
            barrier, inc=1, device_id=(lax.rem(me + d, SETS), lev), device_id_type=MESH
        )
        return 0

    z_peers = [o % LEVELS for o in range(-REACH - 1, REACH + 2) if o]
    for d in z_peers:
        pl.semaphore_signal(
            barrier, inc=1, device_id=(me, lax.rem(lev + d, LEVELS)), device_id_type=MESH
        )
    lax.fori_loop(1, SETS, greet, 0)

    for c in inputs:
        c.wait()
    m_lane = jnp.concatenate([waves[...].astype(F32)] * 4, axis=1)
    m_sub = jnp.broadcast_to(m_lane, (LANES, LANES)).T
    lane8 = lax.broadcasted_iota(jnp.int32, (8, LANES), 1)
    own_m = jnp.sum(jnp.where(lane8[0:1, 0:SETS] == me, m_lane[:, 0:SETS], 0.0), axis=1, keepdims=True)
    degree = lax.broadcasted_iota(jnp.int32, (4, DEG), 1).astype(F32)
    kept = degree <= (DEG - 1.0) - own_m
    rows = jnp.concatenate([spec[0].astype(F32), spec[1].astype(F32)], axis=0)
    rows = jnp.where(kept, rows, 0.0)
    own_s[...] = rows[2:4].astype(BF16)
    group_of = lane8 // 8
    group_masks = [group_of == g for g in range(16)]

    def eight(x):
        pad = jnp.zeros((8 - x.shape[0], DEG), F32)
        return jnp.concatenate([x, pad], axis=0).astype(BF16)

    def product(left, q):
        nat_s[:, 256 * q : 256 * q + 256] = lax.dot_general(
            left,
            table[256 * q : 256 * q + 256, :],
            (((1,), (1,)), ((), ())),
            preferred_element_type=F32,
        )

    def post(stage):
        for w in range(SETS):
            acc = None
            for q in range(10):
                chunk = w if q < 5 else SETS - 1 - w
                at = 256 * q + LANES * (chunk // 16)
                shift = (8 * q - 8 * (chunk % 16)) % LANES
                piece = nat_s[:, at : at + LANES]
                piece = pltpu.roll(piece, shift, 1) if shift else piece
                acc = piece if acc is None else jnp.where(group_masks[q], piece, acc)
            sends[stage, w] = acc.astype(BF16)

    def plane_copy(stage, d):
        to = lax.rem(me + d, SETS)
        return pltpu.make_async_remote_copy(
            src_ref=sends.at[stage, to],
            dst_ref=gets.at[stage, me],
            send_sem=plane_sem.at[stage, 0, d],
            recv_sem=plane_sem.at[stage, 1, d],
            device_id=(to, lev),
            device_id_type=MESH,
        )

    def plane_start(stage):
        def one(d, _):
            plane_copy(stage, d).start()
            return 0

        lax.fori_loop(1, SETS, one, 0, unroll=True)
        gets[stage, me] = sends[stage, me]

    def plane_wait(stage, sent=False):
        def one(d, _):
            origin = lax.rem(me - d + SETS, SETS)
            copy = pltpu.make_async_remote_copy(
                src_ref=sends.at[stage, lax.rem(me + d, SETS)],
                dst_ref=gets.at[stage, origin],
                send_sem=plane_sem.at[stage, 0, d],
                recv_sem=plane_sem.at[stage, 1, d],
                device_id=(origin, lev),
                device_id_type=MESH,
            )
            copy.wait_send() if sent else copy.wait_recv()
            return 0

        lax.fori_loop(1, SETS, one, 0, unroll=True)

    def z_copy(src, dst, sems, i, shift):
        return pltpu.make_async_remote_copy(
            src_ref=src,
            dst_ref=dst,
            send_sem=sems.at[0, i],
            recv_sem=sems.at[1, i],
            device_id=(me, lax.rem(lev + shift, LEVELS)),
            device_id_type=MESH,
        )

    nears = [
        z_copy(own_s, near_s.at[i], near_sem, i, (-o) % LEVELS) for i, o in enumerate(NEAR)
    ]
    fars = [
        z_copy(node_s.at[i], far_s.at[i], far_sem, i, shift)
        for i, shift in enumerate((LEVELS - SPAN, SPAN))
    ]

    t_lane = lax.broadcasted_iota(jnp.int32, (64, LANES), 1).astype(F32)

    def tables(q):
        a_sub = lax.broadcasted_iota(jnp.int32, (ROWS[q], LANES), 0)
        lane = lax.broadcasted_iota(jnp.int32, (ROWS[q], LANES), 1)
        coarse_base = (a_sub * LANES).astype(F32) * m_lane
        coarse_shift = jnp.where(lane < 64, 0.0, 0.25)
        fine_base = m_sub[0:64] * t_lane
        fine_shift = jnp.where(lax.broadcasted_iota(jnp.int32, (64, LANES), 0) < SETS, 0.0, 0.25)

        def one(r, _):
            n = 8 * q + r
            j = 256 * q + 8 * me + r
            length = jnp.full((8, LANES), 20 + 4 * j, jnp.int32).astype(F32)
            inv = 1.0 / length
            turn = (jnp.full((8, LANES), j, jnp.int32).astype(F32) + 0.5) / 5120.0
            planet = 2.0 * cos_turns(turn)
            weight = cos_turns(turn - 0.25) * lax.rsqrt(length)
            pair_s[n, 0] = planet
            pair_s[n, 1] = weight
            length, inv = length[0:1], inv[0:1]
            fine = cos_turns(turns(fine_base, inv, length) + fine_shift).astype(BF16)
            fine_s[n, 0:64] = fine
            fine_s[n, 64:128] = fine
            coarse_s[q][r] = cos_turns(turns(coarse_base, inv, length) - coarse_shift)
            return 0

        lax.fori_loop(0, 8, one, 0, unroll=2)

    scale = 1.0 / math.sqrt(LEVELS)

    def take_lines(stage, count, base):
        wide[...] = gets[stage].astype(F32).reshape(SETS * 8, LANES)
        for k in range(count):
            re = wide[pl.ds(2 * k, SETS, stride=8), :] * scale
            im = wide[pl.ds(2 * k + 1, SETS, stride=8), :] * scale
            lines[base + k] = jnp.concatenate([re, im, -im, re], axis=0).T

    def shown(x, inside):
        count = x.shape[0]
        tail = jnp.where(inside, x[count - 16 :], 0.0)
        return tail if count == 16 else jnp.concatenate([x[: count - 16], tail], axis=0)

    def analyse(field, parts, n, coarse, fine, weight):
        count = coarse.shape[0]
        tend = jnp.concatenate(parts, axis=0).astype(BF16)
        back = lax.dot_general(tend, fine, (((1,), (1,)), ((), ())), preferred_element_type=F32)
        for h, at in enumerate((n, 79 - n)):
            line = jnp.sum(back[h * count : (h + 1) * count] * coarse, axis=0, keepdims=True)
            sums[field, pl.ds(at, 1), :] = line * weight

    def synth(q):
        count = ROWS[q]
        a_sub = lax.broadcasted_iota(jnp.int32, (16, LANES), 0) + (count - 16)
        point = a_sub * LANES + lax.broadcasted_iota(jnp.int32, (16, LANES), 1)

        def one(r, _):
            n = 8 * q + r
            j = 256 * q + 8 * me + r
            coarse = coarse_s[q][r]
            fine = fine_s[n]
            planet = pair_s[n, 0, 0:1]
            parts = [
                lines[k, pl.ds(at, 1), :] * coarse for k in range(2) for at in (n, 79 - n)
            ]
            left = jnp.concatenate(parts, axis=0).astype(BF16)
            grid = jnp.dot(left, fine, preferred_element_type=F32)
            inside = point < (20 + 4 * j)
            first = []
            for h, sign in ((0, 1.0), (1, -1.0)):
                vort = grid[h * count : (h + 1) * count]
                div = shown(grid[(2 + h) * count : (3 + h) * count], inside)
                total = vort + sign * planet
                first.append(total * div)
                grid_s[q][r, h * count : (h + 1) * count] = shown(total * vort, inside)
                grid_s[q][r, (2 + h) * count : (3 + h) * count] = div
            analyse(0, first, n, coarse, fine, -pair_s[n, 1, 0:1])
            return 0

        lax.fori_loop(0, 8, one, 0, unroll=2)

    def finish(q):
        count = ROWS[q]

        def one(r, _):
            n = 8 * q + r
            coarse = coarse_s[q][r]
            fine = fine_s[n]
            left = jnp.concatenate(
                [lines[2, pl.ds(at, 1), :] * coarse for at in (n, 79 - n)], axis=0
            ).astype(BF16)
            col = jnp.dot(left, fine, preferred_element_type=F32)
            second = grid_s[q][r, 0 : 2 * count] - grid_s[q][r, 2 * count : 4 * count] * col
            analyse(1, [second], n, coarse, fine, pair_s[n, 1, 0:1])
            return 0

        lax.fori_loop(0, 8, one, 0, unroll=FINISH)

    own = eight(rows)
    sums[...] = jnp.zeros_like(sums)
    pl.semaphore_wait(barrier, SETS - 1 + len(z_peers))
    for c in nears:
        c.start()

    def products(low, high):
        for q in range(low, high):
            loads[q].wait()
            product(own, q)

    def launch():
        node = rows[2:4]
        last = None
        for i, c in enumerate(nears):
            c.wait_recv()
            term = near_s[i].astype(F32)
            if NEAR[i] == -REACH:
                last = term
            else:
                node += term
        node_s[0] = (node + last).astype(BF16)
        node_s[1] = node.astype(BF16)

    products(0, 10)
    post(0)
    tables(0)
    plane_start(0)
    launch()
    tables(1)
    for c in fars:
        c.start()
    for q in range(2, 5):
        tables(q)
    plane_wait(0)
    take_lines(0, 2, 0)
    for q in range(5):
        synth(q)
    total = node_s[0].astype(F32)
    for i, c in enumerate(fars):
        c.wait_recv()
        total += far_s[i].astype(F32)
    column = eight(total * scale)
    for q in range(10):
        product(column, q)
    post(1)
    plane_start(1)
    plane_wait(1)
    take_lines(1, 1, 2)
    for q in range(5):
        finish(q)
    for k in range(2):
        cols = sums[k].T
        wide[pl.ds(2 * k, SETS, stride=8), :] = cols[0:32] + cols[96:128]
        wide[pl.ds(2 * k + 1, SETS, stride=8), :] = cols[32:64] - cols[64:96]
        wide[pl.ds(2 * k + 4, SETS, stride=8), :] = jnp.zeros((SETS, LANES), F32)
        wide[pl.ds(2 * k + 5, SETS, stride=8), :] = jnp.zeros((SETS, LANES), F32)
    sends[2] = wide[...].reshape(SETS, 8, LANES).astype(BF16)
    plane_start(2)
    plane_wait(2)
    wide[...] = gets[2].astype(F32).reshape(SETS * 8, LANES)
    result = jnp.zeros((8, DEG), F32)
    for q in range(10):
        halves = []
        for b in range(2):
            acc = None
            for g in range(16):
                w = 16 * b + g
                w = w if q < 5 else SETS - 1 - w
                shift = (8 * g - 8 * q) % LANES
                piece = wide[8 * w : 8 * w + 8, :]
                piece = pltpu.roll(piece, shift, 1) if shift else piece
                acc = piece if acc is None else jnp.where(group_masks[g], piece, acc)
            halves.append(acc)
        left = jnp.concatenate(halves, axis=1).astype(BF16)
        result += jnp.dot(
            left, table[256 * q : 256 * q + 256, :], preferred_element_type=F32
        )
    for c in nears + fars:
        c.wait_send()
    for stage in range(3):
        plane_wait(stage, sent=True)
    result = result[0:4]
    result = jnp.where(kept, result, 0.0)
    out[0] = result[0:2].astype(BF16)
    out[1] = result[2:4].astype(BF16)


def body(spectral, legendre, wavenumber):
    anywhere = pl.BlockSpec(memory_space=pl.ANY)
    local = pl.BlockSpec(memory_space=pltpu.VMEM)
    dma = pltpu.SemaphoreType.DMA
    scratch = [
        pltpu.VMEM((2, 2, DEG), BF16),
        pltpu.VMEM((1, SETS), jnp.int32),
        dma((2,)),
        pltpu.VMEM((LATS, DEG), BF16),
        dma((10,)),
        pltpu.VMEM((3, SETS, 8, LANES), BF16),
        pltpu.VMEM((3, SETS, 8, LANES), BF16),
        pltpu.VMEM((SETS * 8, LANES), F32),
        pltpu.VMEM((3, LANES, LANES), F32),
        pltpu.VMEM((2, LANES, LANES), F32),
        pltpu.VMEM((40, LANES, LANES), BF16),
        pltpu.VMEM((40, 2, 8, LANES), F32),
        pltpu.VMEM((8, LATS), F32),
    ]
    scratch += [pltpu.VMEM((8, n, LANES), F32) for n in ROWS]
    scratch += [pltpu.VMEM((8, 4 * n, LANES), F32) for n in ROWS]
    scratch += [
        pltpu.VMEM((2, DEG), BF16),
        pltpu.VMEM((len(NEAR), 2, DEG), BF16),
        pltpu.VMEM((2, 2, DEG), BF16),
        pltpu.VMEM((2, 2, DEG), BF16),
        dma((2, len(NEAR))),
        dma((2, 2)),
        dma((3, 2, SETS)),
    ]
    result = pl.pallas_call(
        kernel,
        out_shape=jax.ShapeDtypeStruct((2, 2, DEG), BF16),
        in_specs=[anywhere, anywhere, anywhere],
        out_specs=local,
        scratch_shapes=scratch,
        compiler_params=pltpu.CompilerParams(
            collective_id=0, has_side_effects=True, vmem_limit_bytes=62_000_000
        ),
    )(spectral.reshape(2, 2, DEG), wavenumber.reshape(1, SETS), legendre.reshape(LATS, DEG))
    return result.reshape(2, 1, 2, 1, DEG)


def solution(mesh):
    in_specs = (P(None, "lev", None, "wave", None), P("wave", None, None), P())
    out_specs = P(None, "lev", None, "wave", None)
    return jax.shard_map(body, mesh=mesh, in_specs=in_specs, out_specs=out_specs, check_vma=False)
```

```python
import functools
import math

import jax
import jax.numpy as jnp
from jax import lax
from jax.experimental import pallas as pl
from jax.experimental.pallas import tpu as pltpu
from jax.sharding import PartitionSpec as P

LATS = 2560
DEG = 1280
SETS = 32
LEVELS = 32
LANES = 128
REACH = 5
SPAN = 2 * REACH + 1
NEAR = [o * side for o in range(REACH, 0, -1) for side in (1, -1)]
FINISH = 4
HALVES = (((0, 1, 2), (0, 1, 2, 7, 8, 9)), ((3, 4), (3, 4, 5, 6)))
PEERS = sorted(
    ((dx, dy, dc) for dx in range(4) for dy in range(4) for dc in range(2) if dx + dy + dc),
    key=lambda p: -(min(p[0], 4 - p[0]) + min(p[1], 4 - p[1])),
)
ROWS = (16, 24, 32, 40, 48)
F32 = jnp.float32
BF16 = jnp.bfloat16
MESH = pl.DeviceIdType.MESH


def cos_turns(f):
    r = f - jnp.round(f)
    y = 0.25 - jnp.abs(r)
    z = y * y
    tau = 2.0 * math.pi
    coef = [(-1.0) ** k * tau ** (2 * k + 1) / math.factorial(2 * k + 1) for k in range(6)]
    acc = jnp.full_like(z, coef[5])
    for c in coef[4::-1]:
        acc = acc * z + c
    return acc * y


def turns(product, inv, length):
    q = jnp.round(product * inv)
    return (product - q * length) * inv


def kernel(spec_in, waves_in, leg, out, *scratch):
    (spec, waves, in_sem, table, table_sem, sends, gets, wide, back_s, lines, sums, fine_s, pair_s, nat_s) = scratch[:14]
    coarse_s = scratch[14:19]
    grid_s = scratch[19:24]
    (own_s, near_s, node_s, far_s, near_sem, far_sem, plane_sem) = scratch[24:]
    me = lax.axis_index("wave")
    lev = lax.axis_index("lev")

    inputs = [
        pltpu.make_async_copy(spec_in, spec, in_sem.at[0]),
        pltpu.make_async_copy(waves_in, waves, in_sem.at[1]),
    ]
    for c in inputs:
        c.start()
    loads = [
        pltpu.make_async_copy(
            leg.at[pl.ds(256 * q, 256)], table.at[pl.ds(256 * q, 256)], table_sem.at[q]
        )
        for q in range(10)
    ]
    for c in loads:
        c.start()

    barrier = pltpu.get_barrier_semaphore()

    def greet(d, _):
        pl.semaphore_signal(
            barrier, inc=1, device_id=(lax.rem(me + d, SETS), lev), device_id_type=MESH
        )
        return 0

    z_peers = [o % LEVELS for o in range(-REACH - 1, REACH + 2) if o]
    for d in z_peers:
        pl.semaphore_signal(
            barrier, inc=1, device_id=(me, lax.rem(lev + d, LEVELS)), device_id_type=MESH
        )
    lax.fori_loop(1, SETS, greet, 0)

    for c in inputs:
        c.wait()
    m_lane = jnp.concatenate([waves[...].astype(F32)] * 4, axis=1)
    m_sub = jnp.broadcast_to(m_lane, (LANES, LANES)).T
    lane8 = lax.broadcasted_iota(jnp.int32, (8, LANES), 1)
    own_m = jnp.sum(jnp.where(lane8[0:1, 0:SETS] == me, m_lane[:, 0:SETS], 0.0), axis=1, keepdims=True)
    degree = lax.broadcasted_iota(jnp.int32, (4, DEG), 1).astype(F32)
    kept = degree <= (DEG - 1.0) - own_m
    rows = jnp.concatenate([spec[0].astype(F32), spec[1].astype(F32)], axis=0)
    rows = jnp.where(kept, rows, 0.0)
    own_s[...] = rows[2:4].astype(BF16)
    group_of = lane8 // 8
    group_masks = [group_of == g for g in range(16)]

    def eight(x):
        pad = jnp.zeros((8 - x.shape[0], DEG), F32)
        return jnp.concatenate([x, pad], axis=0).astype(BF16)

    def product(left, q):
        nat_s[:, 256 * q : 256 * q + 256] = lax.dot_general(
            left,
            table[256 * q : 256 * q + 256, :],
            (((1,), (1,)), ((), ())),
            preferred_element_type=F32,
        )

    def post(stage, chunks):
        for w in range(SETS):
            acc = None
            for q in chunks:
                chunk = w if q < 5 else SETS - 1 - w
                at = 256 * q + LANES * (chunk // 16)
                shift = (8 * q - 8 * (chunk % 16)) % LANES
                piece = nat_s[:, at : at + LANES]
                piece = pltpu.roll(piece, shift, 1) if shift else piece
                acc = piece if acc is None else jnp.where(group_masks[q], piece, acc)
            sends[stage, w] = acc.astype(BF16)

    def parts(sign):
        x, y, c = me // 8, (me // 2) % 4, me % 2
        return (
            [(x + sign * d + 4) % 4 * 8 for d in range(4)],
            [(y + sign * d + 4) % 4 * 2 for d in range(4)],
            [(c + d) % 2 for d in range(2)],
        )

    ahead, behind = parts(1), parts(-1)

    def plane_copy(stage, i, receive):
        dx, dy, dc = PEERS[i]
        to = ahead[0][dx] + ahead[1][dy] + ahead[2][dc]
        origin = behind[0][dx] + behind[1][dy] + behind[2][dc]
        return pltpu.make_async_remote_copy(
            src_ref=sends.at[stage, to],
            dst_ref=gets.at[stage, origin if receive else me],
            send_sem=plane_sem.at[stage, 0, i],
            recv_sem=plane_sem.at[stage, 1, i],
            device_id=(to, lev),
            device_id_type=MESH,
        )

    def plane_start(stage):
        for i in range(len(PEERS)):
            plane_copy(stage, i, False).start()
        gets[stage, me] = sends[stage, me]

    def plane_wait(stage, sent=False):
        for i in range(len(PEERS)):
            copy = plane_copy(stage, i, True)
            copy.wait_send() if sent else copy.wait_recv()

    def z_copy(src, dst, sems, i, shift):
        return pltpu.make_async_remote_copy(
            src_ref=src,
            dst_ref=dst,
            send_sem=sems.at[0, i],
            recv_sem=sems.at[1, i],
            device_id=(me, lax.rem(lev + shift, LEVELS)),
            device_id_type=MESH,
        )

    nears = [
        z_copy(own_s, near_s.at[i], near_sem, i, (-o) % LEVELS) for i, o in enumerate(NEAR)
    ]
    fars = [
        z_copy(node_s.at[i], far_s.at[i], far_sem, i, shift)
        for i, shift in enumerate((LEVELS - SPAN, SPAN))
    ]

    t_lane = lax.broadcasted_iota(jnp.int32, (64, LANES), 1).astype(F32)

    def tables(q):
        a_sub = lax.broadcasted_iota(jnp.int32, (ROWS[q], LANES), 0)
        lane = lax.broadcasted_iota(jnp.int32, (ROWS[q], LANES), 1)
        coarse_base = (a_sub * LANES).astype(F32) * m_lane
        coarse_shift = jnp.where(lane < 64, 0.0, 0.25)
        fine_base = m_sub[0:64] * t_lane
        fine_shift = jnp.where(lax.broadcasted_iota(jnp.int32, (64, LANES), 0) < SETS, 0.0, 0.25)

        def one(r, _):
            n = 8 * q + r
            j = 256 * q + 8 * me + r
            length = jnp.full((8, LANES), 20 + 4 * j, jnp.int32).astype(F32)
            inv = 1.0 / length
            turn = (jnp.full((8, LANES), j, jnp.int32).astype(F32) + 0.5) / 5120.0
            planet = 2.0 * cos_turns(turn)
            weight = cos_turns(turn - 0.25) * lax.rsqrt(length)
            pair_s[n, 0] = planet
            pair_s[n, 1] = weight
            length, inv = length[0:1], inv[0:1]
            fine = cos_turns(turns(fine_base, inv, length) + fine_shift).astype(BF16)
            fine_s[n, 0:64] = fine
            fine_s[n, 64:128] = fine
            coarse_s[q][r] = cos_turns(turns(coarse_base, inv, length) - coarse_shift)
            return 0

        lax.fori_loop(0, 8, one, 0, unroll=2)

    scale = 1.0 / math.sqrt(LEVELS)

    def take_lines(stage, count, base):
        wide[...] = gets[stage].astype(F32).reshape(SETS * 8, LANES)
        for k in range(count):
            re = wide[pl.ds(2 * k, SETS, stride=8), :] * scale
            im = wide[pl.ds(2 * k + 1, SETS, stride=8), :] * scale
            lines[base + k] = jnp.concatenate([re, im, -im, re], axis=0).T

    def shown(x, inside):
        count = x.shape[0]
        tail = jnp.where(inside, x[count - 16 :], 0.0)
        return tail if count == 16 else jnp.concatenate([x[: count - 16], tail], axis=0)

    def analyse(field, parts, n, coarse, fine, weight):
        count = coarse.shape[0]
        tend = jnp.concatenate(parts, axis=0).astype(BF16)
        back = lax.dot_general(tend, fine, (((1,), (1,)), ((), ())), preferred_element_type=F32)
        for h, at in enumerate((n, 79 - n)):
            line = jnp.sum(back[h * count : (h + 1) * count] * coarse, axis=0, keepdims=True)
            sums[field, pl.ds(at, 1), :] = line * weight

    def synth(q):
        count = ROWS[q]
        a_sub = lax.broadcasted_iota(jnp.int32, (16, LANES), 0) + (count - 16)
        point = a_sub * LANES + lax.broadcasted_iota(jnp.int32, (16, LANES), 1)

        def one(r, _):
            n = 8 * q + r
            j = 256 * q + 8 * me + r
            coarse = coarse_s[q][r]
            fine = fine_s[n]
            planet = pair_s[n, 0, 0:1]
            parts = [
                lines[k, pl.ds(at, 1), :] * coarse for k in range(2) for at in (n, 79 - n)
            ]
            left = jnp.concatenate(parts, axis=0).astype(BF16)
            grid = jnp.dot(left, fine, preferred_element_type=F32)
            inside = point < (20 + 4 * j)
            first = []
            for h, sign in ((0, 1.0), (1, -1.0)):
                vort = grid[h * count : (h + 1) * count]
                div = shown(grid[(2 + h) * count : (3 + h) * count], inside)
                total = vort + sign * planet
                first.append(total * div)
                grid_s[q][r, h * count : (h + 1) * count] = shown(total * vort, inside)
                grid_s[q][r, (2 + h) * count : (3 + h) * count] = div
            analyse(0, first, n, coarse, fine, -pair_s[n, 1, 0:1])
            return 0

        lax.fori_loop(0, 8, one, 0, unroll=2)

    def finish(q):
        count = ROWS[q]

        def one(r, _):
            n = 8 * q + r
            coarse = coarse_s[q][r]
            fine = fine_s[n]
            left = jnp.concatenate(
                [lines[2, pl.ds(at, 1), :] * coarse for at in (n, 79 - n)], axis=0
            ).astype(BF16)
            col = jnp.dot(left, fine, preferred_element_type=F32)
            second = grid_s[q][r, 0 : 2 * count] - grid_s[q][r, 2 * count : 4 * count] * col
            analyse(1, [second], n, coarse, fine, pair_s[n, 1, 0:1])
            return 0

        lax.fori_loop(0, 8, one, 0, unroll=FINISH)

    def spread(k):
        cols = sums[k].T
        back_s[pl.ds(2 * k, SETS, stride=8), :] = cols[0:32] + cols[96:128]
        back_s[pl.ds(2 * k + 1, SETS, stride=8), :] = cols[32:64] - cols[64:96]

    own = eight(rows)
    back_s[...] = jnp.zeros_like(back_s)
    sums[...] = jnp.zeros_like(sums)
    pl.semaphore_wait(barrier, SETS - 1 + len(z_peers))
    for c in nears:
        c.start()

    def products(low, high):
        for q in range(low, high):
            loads[q].wait()
            product(own, q)

    def launch():
        node = rows[2:4]
        last = None
        for i, c in enumerate(nears):
            c.wait_recv()
            term = near_s[i].astype(F32)
            if NEAR[i] == -REACH:
                last = term
            else:
                node += term
        node_s[0] = (node + last).astype(BF16)
        node_s[1] = node.astype(BF16)

    products(0, 10)
    post(0, range(10))
    tables(0)
    plane_start(0)
    launch()
    tables(1)
    for c in fars:
        c.start()
    for q in range(2, 5):
        tables(q)
    plane_wait(0)
    take_lines(0, 2, 0)
    for q in range(5):
        synth(q)
    spread(0)
    total = node_s[0].astype(F32)
    for i, c in enumerate(fars):
        c.wait_recv()
        total += far_s[i].astype(F32)
    column = eight(total * scale)
    for half, (_, chunks) in enumerate(HALVES):
        for q in chunks:
            product(column, q)
        post(1 + half, chunks)
        plane_start(1 + half)
    for half, (own_lats, _) in enumerate(HALVES):
        plane_wait(1 + half)
        take_lines(1 + half, 1, 2)
        for q in own_lats:
            finish(q)
        spread(1)
        sends[3 + half] = back_s[...].reshape(SETS, 8, LANES).astype(BF16)
        plane_start(3 + half)
    for c in nears + fars:
        c.wait_send()
    for stage in range(3):
        plane_wait(stage, sent=True)
    result = jnp.zeros((8, DEG), F32)
    for half, (_, chunks) in enumerate(HALVES):
        plane_wait(3 + half, sent=True)
        plane_wait(3 + half)
        wide[...] = gets[3 + half].astype(F32).reshape(SETS * 8, LANES)
        for q in chunks:
            halves = []
            for b in range(2):
                acc = None
                for g in range(16):
                    w = 16 * b + g
                    w = w if q < 5 else SETS - 1 - w
                    shift = (8 * g - 8 * q) % LANES
                    piece = wide[8 * w : 8 * w + 8, :]
                    piece = pltpu.roll(piece, shift, 1) if shift else piece
                    acc = piece if acc is None else jnp.where(group_masks[g], piece, acc)
                halves.append(acc)
            left = jnp.concatenate(halves, axis=1).astype(BF16)
            result += jnp.dot(
                left, table[256 * q : 256 * q + 256, :], preferred_element_type=F32
            )
    result = result[0:4]
    result = jnp.where(kept, result, 0.0)
    out[0] = result[0:2].astype(BF16)
    out[1] = result[2:4].astype(BF16)


def body(spectral, legendre, wavenumber):
    anywhere = pl.BlockSpec(memory_space=pl.ANY)
    local = pl.BlockSpec(memory_space=pltpu.VMEM)
    dma = pltpu.SemaphoreType.DMA
    scratch = [
        pltpu.VMEM((2, 2, DEG), BF16),
        pltpu.VMEM((1, SETS), jnp.int32),
        dma((2,)),
        pltpu.VMEM((LATS, DEG), BF16),
        dma((10,)),
        pltpu.VMEM((5, SETS, 8, LANES), BF16),
        pltpu.VMEM((5, SETS, 8, LANES), BF16),
        pltpu.VMEM((SETS * 8, LANES), F32),
        pltpu.VMEM((SETS * 8, LANES), F32),
        pltpu.VMEM((3, LANES, LANES), F32),
        pltpu.VMEM((2, LANES, LANES), F32),
        pltpu.VMEM((40, LANES, LANES), BF16),
        pltpu.VMEM((40, 2, 8, LANES), F32),
        pltpu.VMEM((8, LATS), F32),
    ]
    scratch += [pltpu.VMEM((8, n, LANES), F32) for n in ROWS]
    scratch += [pltpu.VMEM((8, 4 * n, LANES), F32) for n in ROWS]
    scratch += [
        pltpu.VMEM((2, DEG), BF16),
        pltpu.VMEM((len(NEAR), 2, DEG), BF16),
        pltpu.VMEM((2, 2, DEG), BF16),
        pltpu.VMEM((2, 2, DEG), BF16),
        dma((2, len(NEAR))),
        dma((2, 2)),
        dma((5, 2, SETS)),
    ]
    result = pl.pallas_call(
        kernel,
        out_shape=jax.ShapeDtypeStruct((2, 2, DEG), BF16),
        in_specs=[anywhere, anywhere, anywhere],
        out_specs=local,
        scratch_shapes=scratch,
        compiler_params=pltpu.CompilerParams(
            collective_id=0, has_side_effects=True, vmem_limit_bytes=62_000_000
        ),
    )(spectral.reshape(2, 2, DEG), wavenumber.reshape(1, SETS), legendre.reshape(LATS, DEG))
    return result.reshape(2, 1, 2, 1, DEG)


def solution(mesh):
    in_specs = (P(None, "lev", None, "wave", None), P("wave", None, None), P())
    out_specs = P(None, "lev", None, "wave", None)
    return jax.shard_map(body, mesh=mesh, in_specs=in_specs, out_specs=out_specs, check_vma=False)
```

```python
import functools
import math

import jax
import jax.numpy as jnp
from jax import lax
from jax.experimental import pallas as pl
from jax.experimental.pallas import tpu as pltpu
from jax.sharding import PartitionSpec as P

LATS = 2560
DEG = 1280
SETS = 32
LEVELS = 32
LANES = 128
REACH = 5
SPAN = 2 * REACH + 1
NEAR = [o * side for o in range(REACH, 0, -1) for side in (1, -1)]
FINISH = 4
HALVES = (((0, 1, 2), (0, 1, 2, 7, 8, 9)), ((3, 4), (3, 4, 5, 6)))
PEERS = sorted(
    ((dx, dy, dc) for dx in range(4) for dy in range(4) for dc in range(2) if dx + dy + dc),
    key=lambda p: -(min(p[0], 4 - p[0]) + min(p[1], 4 - p[1])),
)
ROWS = (16, 24, 32, 40, 48)
F32 = jnp.float32
BF16 = jnp.bfloat16
MESH = pl.DeviceIdType.MESH


def cos_turns(f):
    r = f - jnp.round(f)
    y = 0.25 - jnp.abs(r)
    z = y * y
    tau = 2.0 * math.pi
    coef = [(-1.0) ** k * tau ** (2 * k + 1) / math.factorial(2 * k + 1) for k in range(6)]
    acc = jnp.full_like(z, coef[5])
    for c in coef[4::-1]:
        acc = acc * z + c
    return acc * y


def turns(product, inv, length):
    q = jnp.round(product * inv)
    return (product - q * length) * inv


def kernel(spec_in, waves_in, leg, out, *scratch):
    (spec, waves, in_sem, table, table_sem, sends, gets, wide, back_s, lines, sums, fine_s, pair_s, nat_s) = scratch[:14]
    coarse_s = scratch[14:19]
    grid_s = scratch[19:24]
    (own_s, near_s, node_s, far_s, near_sem, far_sem, plane_sem) = scratch[24:]
    me = lax.axis_index("wave")
    lev = lax.axis_index("lev")

    inputs = [
        pltpu.make_async_copy(spec_in, spec, in_sem.at[0]),
        pltpu.make_async_copy(waves_in, waves, in_sem.at[1]),
    ]
    for c in inputs:
        c.start()
    loads = [
        pltpu.make_async_copy(
            leg.at[pl.ds(256 * q, 256)], table.at[pl.ds(256 * q, 256)], table_sem.at[q]
        )
        for q in range(10)
    ]
    for c in loads:
        c.start()

    barrier = pltpu.get_barrier_semaphore()

    def parts(sign):
        x, y, c = me // 8, (me // 2) % 4, me % 2
        return (
            [(x + sign * d + 4) % 4 * 8 for d in range(4)],
            [(y + sign * d + 4) % 4 * 2 for d in range(4)],
            [(c + d) % 2 for d in range(2)],
        )

    ahead, behind = parts(1), parts(-1)

    z_peers = [o % LEVELS for o in range(-REACH - 1, REACH + 2) if o]
    for d in z_peers:
        pl.semaphore_signal(
            barrier, inc=1, device_id=(me, lax.rem(lev + d, LEVELS)), device_id_type=MESH
        )
    for dx, dy, dc in PEERS:
        to = ahead[0][dx] + ahead[1][dy] + ahead[2][dc]
        pl.semaphore_signal(barrier, inc=1, device_id=(to, lev), device_id_type=MESH)

    for c in inputs:
        c.wait()
    m_lane = jnp.concatenate([waves[...].astype(F32)] * 4, axis=1)
    m_sub = jnp.broadcast_to(m_lane, (LANES, LANES)).T
    lane8 = lax.broadcasted_iota(jnp.int32, (8, LANES), 1)
    own_m = jnp.sum(jnp.where(lane8[0:1, 0:SETS] == me, m_lane[:, 0:SETS], 0.0), axis=1, keepdims=True)
    degree = lax.broadcasted_iota(jnp.int32, (4, DEG), 1).astype(F32)
    kept = degree <= (DEG - 1.0) - own_m
    rows = jnp.concatenate([spec[0].astype(F32), spec[1].astype(F32)], axis=0)
    rows = jnp.where(kept, rows, 0.0)
    own_s[...] = rows[2:4].astype(BF16)
    group_of = lane8 // 8
    group_masks = [group_of == g for g in range(16)]

    def eight(x):
        pad = jnp.zeros((8 - x.shape[0], DEG), F32)
        return jnp.concatenate([x, pad], axis=0).astype(BF16)

    def product(left, q):
        nat_s[:, 256 * q : 256 * q + 256] = lax.dot_general(
            left,
            table[256 * q : 256 * q + 256, :],
            (((1,), (1,)), ((), ())),
            preferred_element_type=F32,
        )

    def post(stage, chunks):
        for w in range(SETS):
            acc = None
            for q in chunks:
                chunk = w if q < 5 else SETS - 1 - w
                at = 256 * q + LANES * (chunk // 16)
                shift = (8 * q - 8 * (chunk % 16)) % LANES
                piece = nat_s[:, at : at + LANES]
                piece = pltpu.roll(piece, shift, 1) if shift else piece
                acc = piece if acc is None else jnp.where(group_masks[q], piece, acc)
            sends[stage, w] = acc.astype(BF16)

    def plane_copy(stage, i, receive):
        dx, dy, dc = PEERS[i]
        to = ahead[0][dx] + ahead[1][dy] + ahead[2][dc]
        origin = behind[0][dx] + behind[1][dy] + behind[2][dc]
        return pltpu.make_async_remote_copy(
            src_ref=sends.at[stage, to],
            dst_ref=gets.at[stage, origin if receive else me],
            send_sem=plane_sem.at[stage, 0, i],
            recv_sem=plane_sem.at[stage, 1, i],
            device_id=(to, lev),
            device_id_type=MESH,
        )

    def plane_start(stage):
        for i in range(len(PEERS)):
            plane_copy(stage, i, False).start()
        gets[stage, me] = sends[stage, me]

    def plane_wait(stage, sent=False):
        for i in range(len(PEERS)):
            copy = plane_copy(stage, i, True)
            copy.wait_send() if sent else copy.wait_recv()

    def z_copy(src, dst, sems, i, shift):
        return pltpu.make_async_remote_copy(
            src_ref=src,
            dst_ref=dst,
            send_sem=sems.at[0, i],
            recv_sem=sems.at[1, i],
            device_id=(me, lax.rem(lev + shift, LEVELS)),
            device_id_type=MESH,
        )

    nears = [
        z_copy(own_s, near_s.at[i], near_sem, i, (-o) % LEVELS) for i, o in enumerate(NEAR)
    ]
    fars = [
        z_copy(node_s.at[i], far_s.at[i], far_sem, i, shift)
        for i, shift in enumerate((LEVELS - SPAN, SPAN))
    ]

    t_lane = lax.broadcasted_iota(jnp.int32, (64, LANES), 1).astype(F32)

    def tables(q):
        a_sub = lax.broadcasted_iota(jnp.int32, (ROWS[q], LANES), 0)
        lane = lax.broadcasted_iota(jnp.int32, (ROWS[q], LANES), 1)
        coarse_base = (a_sub * LANES).astype(F32) * m_lane
        coarse_shift = jnp.where(lane < 64, 0.0, 0.25)
        fine_base = m_sub[0:64] * t_lane
        fine_shift = jnp.where(lax.broadcasted_iota(jnp.int32, (64, LANES), 0) < SETS, 0.0, 0.25)

        def one(r, _):
            n = 8 * q + r
            j = 256 * q + 8 * me + r
            length = jnp.full((8, LANES), 20 + 4 * j, jnp.int32).astype(F32)
            inv = 1.0 / length
            turn = (jnp.full((8, LANES), j, jnp.int32).astype(F32) + 0.5) / 5120.0
            planet = 2.0 * cos_turns(turn)
            weight = cos_turns(turn - 0.25) * lax.rsqrt(length)
            pair_s[n, 0] = planet
            pair_s[n, 1] = weight
            length, inv = length[0:1], inv[0:1]
            fine = cos_turns(turns(fine_base, inv, length) + fine_shift).astype(BF16)
            fine_s[n, 0:64] = fine
            fine_s[n, 64:128] = fine
            coarse_s[q][r] = cos_turns(turns(coarse_base, inv, length) - coarse_shift)
            return 0

        lax.fori_loop(0, 8, one, 0, unroll=2)

    scale = 1.0 / math.sqrt(LEVELS)

    def take_lines(stage, count, base):
        wide[...] = gets[stage].astype(F32).reshape(SETS * 8, LANES)
        for k in range(count):
            re = wide[pl.ds(2 * k, SETS, stride=8), :] * scale
            im = wide[pl.ds(2 * k + 1, SETS, stride=8), :] * scale
            lines[base + k] = jnp.concatenate([re, im, -im, re], axis=0).T

    def shown(x, inside):
        count = x.shape[0]
        tail = jnp.where(inside, x[count - 16 :], 0.0)
        return tail if count == 16 else jnp.concatenate([x[: count - 16], tail], axis=0)

    def analyse(field, parts, n, coarse, fine, weight):
        count = coarse.shape[0]
        tend = jnp.concatenate(parts, axis=0).astype(BF16)
        back = lax.dot_general(tend, fine, (((1,), (1,)), ((), ())), preferred_element_type=F32)
        for h, at in enumerate((n, 79 - n)):
            line = jnp.sum(back[h * count : (h + 1) * count] * coarse, axis=0, keepdims=True)
            sums[field, pl.ds(at, 1), :] = line * weight

    def synth(q):
        count = ROWS[q]
        a_sub = lax.broadcasted_iota(jnp.int32, (16, LANES), 0) + (count - 16)
        point = a_sub * LANES + lax.broadcasted_iota(jnp.int32, (16, LANES), 1)

        def one(r, _):
            n = 8 * q + r
            j = 256 * q + 8 * me + r
            coarse = coarse_s[q][r]
            fine = fine_s[n]
            planet = pair_s[n, 0, 0:1]
            parts = [
                lines[k, pl.ds(at, 1), :] * coarse for k in range(2) for at in (n, 79 - n)
            ]
            left = jnp.concatenate(parts, axis=0).astype(BF16)
            grid = jnp.dot(left, fine, preferred_element_type=F32)
            inside = point < (20 + 4 * j)
            first = []
            for h, sign in ((0, 1.0), (1, -1.0)):
                vort = grid[h * count : (h + 1) * count]
                div = shown(grid[(2 + h) * count : (3 + h) * count], inside)
                total = vort + sign * planet
                first.append(total * div)
                grid_s[q][r, h * count : (h + 1) * count] = shown(total * vort, inside)
                grid_s[q][r, (2 + h) * count : (3 + h) * count] = div
            analyse(0, first, n, coarse, fine, -pair_s[n, 1, 0:1])
            return 0

        lax.fori_loop(0, 8, one, 0, unroll=2)

    def finish(q):
        count = ROWS[q]

        def one(r, _):
            n = 8 * q + r
            coarse = coarse_s[q][r]
            fine = fine_s[n]
            left = jnp.concatenate(
                [lines[2, pl.ds(at, 1), :] * coarse for at in (n, 79 - n)], axis=0
            ).astype(BF16)
            col = jnp.dot(left, fine, preferred_element_type=F32)
            second = grid_s[q][r, 0 : 2 * count] - grid_s[q][r, 2 * count : 4 * count] * col
            analyse(1, [second], n, coarse, fine, pair_s[n, 1, 0:1])
            return 0

        lax.fori_loop(0, 8, one, 0, unroll=FINISH)

    def spread(k):
        cols = sums[k].T
        back_s[pl.ds(2 * k, SETS, stride=8), :] = cols[0:32] + cols[96:128]
        back_s[pl.ds(2 * k + 1, SETS, stride=8), :] = cols[32:64] - cols[64:96]

    own = eight(rows)
    pl.semaphore_wait(barrier, SETS - 1 + len(z_peers))
    for c in nears:
        c.start()

    def products(low, high):
        for q in range(low, high):
            loads[q].wait()
            product(own, q)

    def launch():
        node = rows[2:4]
        last = None
        for i, c in enumerate(nears):
            c.wait_recv()
            term = near_s[i].astype(F32)
            if NEAR[i] == -REACH:
                last = term
            else:
                node += term
        node_s[0] = (node + last).astype(BF16)
        node_s[1] = node.astype(BF16)

    products(0, 10)
    post(0, range(10))
    tables(0)
    plane_start(0)
    launch()
    back_s[...] = jnp.zeros_like(back_s)
    sums[...] = jnp.zeros_like(sums)
    for c in fars:
        c.start()
    for q in range(1, 5):
        tables(q)
    plane_wait(0)
    take_lines(0, 2, 0)
    for q in range(5):
        synth(q)
    spread(0)
    total = node_s[0].astype(F32)
    for i, c in enumerate(fars):
        c.wait_recv()
        total += far_s[i].astype(F32)
    column = eight(total * scale)
    for half, (_, chunks) in enumerate(HALVES):
        for q in chunks:
            product(column, q)
        post(1 + half, chunks)
        plane_start(1 + half)
    for half, (own_lats, _) in enumerate(HALVES):
        plane_wait(1 + half)
        take_lines(1 + half, 1, 2)
        for q in own_lats:
            finish(q)
        spread(1)
        sends[3 + half] = back_s[...].reshape(SETS, 8, LANES).astype(BF16)
        plane_start(3 + half)
    for c in nears + fars:
        c.wait_send()
    for stage in range(3):
        plane_wait(stage, sent=True)
    result = jnp.zeros((8, DEG), F32)
    for half, (_, chunks) in enumerate(HALVES):
        plane_wait(3 + half, sent=True)
        plane_wait(3 + half)
        wide[...] = gets[3 + half].astype(F32).reshape(SETS * 8, LANES)
        for q in chunks:
            halves = []
            for b in range(2):
                acc = None
                for g in range(16):
                    w = 16 * b + g
                    w = w if q < 5 else SETS - 1 - w
                    shift = (8 * g - 8 * q) % LANES
                    piece = wide[8 * w : 8 * w + 8, :]
                    piece = pltpu.roll(piece, shift, 1) if shift else piece
                    acc = piece if acc is None else jnp.where(group_masks[g], piece, acc)
                halves.append(acc)
            left = jnp.concatenate(halves, axis=1).astype(BF16)
            result += jnp.dot(
                left, table[256 * q : 256 * q + 256, :], preferred_element_type=F32
            )
    result = result[0:4]
    result = jnp.where(kept, result, 0.0)
    out[0] = result[0:2].astype(BF16)
    out[1] = result[2:4].astype(BF16)


def body(spectral, legendre, wavenumber):
    anywhere = pl.BlockSpec(memory_space=pl.ANY)
    local = pl.BlockSpec(memory_space=pltpu.VMEM)
    dma = pltpu.SemaphoreType.DMA
    scratch = [
        pltpu.VMEM((2, 2, DEG), BF16),
        pltpu.VMEM((1, SETS), jnp.int32),
        dma((2,)),
        pltpu.VMEM((LATS, DEG), BF16),
        dma((10,)),
        pltpu.VMEM((5, SETS, 8, LANES), BF16),
        pltpu.VMEM((5, SETS, 8, LANES), BF16),
        pltpu.VMEM((SETS * 8, LANES), F32),
        pltpu.VMEM((SETS * 8, LANES), F32),
        pltpu.VMEM((3, LANES, LANES), F32),
        pltpu.VMEM((2, LANES, LANES), F32),
        pltpu.VMEM((40, LANES, LANES), BF16),
        pltpu.VMEM((40, 2, 8, LANES), F32),
        pltpu.VMEM((8, LATS), F32),
    ]
    scratch += [pltpu.VMEM((8, n, LANES), F32) for n in ROWS]
    scratch += [pltpu.VMEM((8, 4 * n, LANES), F32) for n in ROWS]
    scratch += [
        pltpu.VMEM((2, DEG), BF16),
        pltpu.VMEM((len(NEAR), 2, DEG), BF16),
        pltpu.VMEM((2, 2, DEG), BF16),
        pltpu.VMEM((2, 2, DEG), BF16),
        dma((2, len(NEAR))),
        dma((2, 2)),
        dma((5, 2, SETS)),
    ]
    result = pl.pallas_call(
        kernel,
        out_shape=jax.ShapeDtypeStruct((2, 2, DEG), BF16),
        in_specs=[anywhere, anywhere, anywhere],
        out_specs=local,
        scratch_shapes=scratch,
        compiler_params=pltpu.CompilerParams(
            collective_id=0, has_side_effects=True, vmem_limit_bytes=62_000_000
        ),
    )(spectral.reshape(2, 2, DEG), wavenumber.reshape(1, SETS), legendre.reshape(LATS, DEG))
    return result.reshape(2, 1, 2, 1, DEG)


def solution(mesh):
    in_specs = (P(None, "lev", None, "wave", None), P("wave", None, None), P())
    out_specs = P(None, "lev", None, "wave", None)
    return jax.shard_map(body, mesh=mesh, in_specs=in_specs, out_specs=out_specs, check_vma=False)
```
